32 devices in a mesh: seq: 8 (over z, core), feat: 4 (over y, x).
Axes of the slice: x: 2, y: 2, z: 4, core: 2. Of those that a mesh axis runs over, the one named last changes fastest.
Arguments:
- layer_inputs: bfloat16 [64, 256, 8192], P('seq', None, 'feat'), may hold values from -6 to 6
- out_grads: bfloat16 [64, 256, 28672], P('seq', None, 'feat'), may hold values from -6 to 6
- lengths: int32 [64], P('seq'), may hold values from 1 to 256, 10240 in all
- row_order: int32 [64], P('seq'), may hold values from 0 to 63, each once
- query_in: bfloat16 [8192, 512], P('feat'), may hold values from -0.005859375 to 0.005859375
- query_out: bfloat16 [28672, 512], P('feat'), may hold values from -0.0029296875 to 0.0029296875
Outputs:
- scores: float32 [64, 16], P('seq')
The draws below stay inside these ranges and needn't reach their ends.
Inputs may be any that keep to these rules, and one draw needn't show every extreme that they name: `lengths`: slots at or past a sequence's length hold padding. `row_order`: each sequence number appears exactly once.
All inputs are finite; a program needn't handle non-finite values. No bound on the sum of `lengths` on one device may be relied on, other than what follows from the above.
Results may differ from the reference program's by a relative error of at most 0.018.
Values may be sent and summed in bfloat16 or wider, within the bound.
No kernel may reach another device: no remote copies, remote signals or barrier semaphores. Data moves between devices by JAX's collectives and lax.ppermute only.
A program may use at most 128 MiB of HBM per device.

```python
import math
import jax
import jax.numpy as jnp
import numpy as np
from jax import lax

D = 8192
FF = 28672
Q = 16
R = 32
LEN = 256
SEQ_DEV = 8
SEQS = 64
FEAT_GROUPS = 4
N_SEQ = 8


def block_scale(rng, extent, split, low, top_value):
    factor_of, own = 1.0, jax.random.fold_in(rng, 6)
    for dim, shards_of in split:
        draws = jnp.exp(jax.random.uniform(jax.random.fold_in(own, dim), (shards_of,), jnp.float32, low / len(split), top_value / len(split)))
        factor_of = factor_of * jnp.repeat(draws, extent[dim] // shards_of).reshape([-1 if axis == dim else 1 for axis in range(len(extent))])
    return factor_of


def profile(count, total, limit, lean):
    loads = [(1 << 20) // math.isqrt(standing ** lean) + 1 for standing in range(2, count + 1)]
    spare, holding = total - limit - (count - 1), [1] * (count - 1)
    while spare > 0:
        free = [i for i in range(count - 1) if holding[i] < limit]
        mass, budget = sum([loads[i] for i in free]), spare
        for i in free:
            addition = min(limit - holding[i], max(1, budget * loads[i] // mass), spare)
            holding[i] = holding[i] + addition
            spare = spare - addition
    return np.array([limit] + holding)


def uneven_parts(stream_key, count, total, limit, lean):
    if count == 2:
        one = jax.random.randint(stream_key, (), max(1, total - limit), min(limit, total - 1) + 1)
        return jnp.stack([one, total - one])
    tallies = jnp.asarray(profile(count, total, limit, lean), jnp.int32)
    twos = (count - 1) // 2
    giver, sink = tallies[1:1 + 2 * twos:2], tallies[2:2 + 2 * twos:2]
    slack = jnp.minimum(giver - 1, limit - sink)
    passed = jax.random.randint(jax.random.fold_in(stream_key, 1), (twos,), 0, 1 << 20) % (slack + 1)
    tallies = tallies.at[1:1 + 2 * twos:2].set(giver - passed).at[2:2 + 2 * twos:2].set(sink + passed)
    return tallies[jax.random.permutation(jax.random.fold_in(stream_key, 2), count)]


def bell_draw(key, shape, spread, most, shards=(), kind=jnp.bfloat16):
    level = block_scale(key, shape, shards, -0.22, 0.18) if shards else 1.0
    array = jax.random.normal(key, shape, jnp.float32) * spread * level
    return jnp.minimum(jnp.maximum(array, -most), most).astype(kind)


def setup_inputs(seed: int = 0) -> dict:
    arg_keys = jax.random.split(jax.random.key(seed), 7)
    layer_inputs = bell_draw(arg_keys[0], (SEQS, LEN, D), 1.0, 6.0, ((0, 8), (2, 4)))
    out_grads = bell_draw(arg_keys[1], (SEQS, LEN, FF), 1.0, 6.0, ((0, 8), (2, 4)))
    lengths = uneven_parts(arg_keys[2], SEQS, SEQ_DEV * N_SEQ * LEN * 5 // 8, LEN, 2).astype(jnp.int32)
    row_order = jax.random.permutation(arg_keys[3], SEQS).astype(jnp.int32)
    query_in = bell_draw(arg_keys[4], (D, Q * R), (D * 128) ** -0.5, 0.005859375, ((0, 4),))
    query_out = bell_draw(arg_keys[5], (FF, Q * R), (FF * 128) ** -0.5, 0.0029296875, ((0, 4),))
    return dict(layer_inputs=layer_inputs, out_grads=out_grads, lengths=lengths, row_order=row_order, query_in=query_in, query_out=query_out)


def reference(layer_inputs, out_grads, lengths, row_order, query_in, query_out):
    row_total = SEQS * LEN
    columns = Q * R
    width_in = D // FEAT_GROUPS
    width_out = FF // FEAT_GROUPS
    flat_in = layer_inputs.reshape(row_total, D)
    flat_out = out_grads.reshape(row_total, FF)

    def add_block(shard_index, running):
        shard_index = jnp.asarray(shard_index).astype(jnp.int32)
        part_in = lax.dynamic_slice_in_dim(flat_in, shard_index * width_in, width_in, 1)
        part_out = lax.dynamic_slice_in_dim(flat_out, shard_index * width_out, width_out, 1)
        factor_in = lax.dynamic_slice_in_dim(query_in, shard_index * width_in, width_in, 0)
        factor_out = lax.dynamic_slice_in_dim(query_out, shard_index * width_out, width_out, 0)
        block_terms = jnp.concatenate(
            [jnp.dot(part_in, factor_in, preferred_element_type=jnp.float32),
             jnp.dot(part_out, factor_out, preferred_element_type=jnp.float32)], axis=1).astype(jnp.bfloat16)
        block_terms = lax.optimization_barrier(block_terms)
        return running + block_terms.astype(jnp.float32)

    projected = lax.fori_loop(0, FEAT_GROUPS, add_block, jnp.zeros((row_total, 2 * columns), jnp.float32))
    products = (projected[:, :columns] * projected[:, columns:]).reshape(SEQS, LEN, columns)
    is_live = (jnp.arange(LEN, dtype=jnp.int32)[None, :] < lengths[:, None]).astype(jnp.float32)
    seq_sums = jnp.sum(products * is_live[:, :, None], axis=1)
    seq_scores = seq_sums.reshape(SEQS, Q, R).sum(axis=2)
    return jnp.take(seq_scores, row_order, axis=0)
```

```python
import functools

import jax
import jax.numpy as jnp
from jax import lax
from jax.experimental import pallas as pl
from jax.experimental.pallas import tpu as pltpu
from jax.sharding import PartitionSpec as P

Q = 16
R = 32
LANES = 128


def matmul_kernel(side_ref, x_ref, w_ref, o_ref):
    o_ref[...] = jnp.dot(x_ref[...], w_ref[...], preferred_element_type=jnp.float32).astype(o_ref.dtype)


def half_matmul(rows, weights, side, tile):
    total, depth = rows.shape
    columns = weights.shape[1]
    half = total // 2
    blocks = half // tile
    return pl.pallas_call(
        matmul_kernel,
        grid_spec=pltpu.PrefetchScalarGridSpec(
            num_scalar_prefetch=1,
            grid=(blocks,),
            in_specs=[
                pl.BlockSpec((tile, depth), lambda i, side: (i + side[0] * blocks, 0)),
                pl.BlockSpec(memory_space=pltpu.VMEM),
            ],
            out_specs=pl.BlockSpec((tile, columns), lambda i, side: (i, 0)),
        ),
        out_shape=jax.ShapeDtypeStruct((half, columns), jnp.bfloat16),
        compiler_params=pltpu.CompilerParams(vmem_limit_bytes=24 << 20),
        cost_estimate=pl.CostEstimate(
            flops=2 * half * depth * columns,
            bytes_accessed=2 * half * (depth + columns),
            transcendentals=0,
        ),
    )(side, pltpu.with_memory_space_constraint(rows, pltpu.HBM), weights)


def score_kernel(seq_dev, devices, side_ref, len_ref, a_ref, ar_ref, b_ref, br_ref, o_ref, acc):
    i = pl.program_id(0)
    count = pl.num_programs(0)
    seq = side_ref[0] * count + i

    @pl.when(i == 0)
    def _():
        acc[...] = jnp.zeros_like(acc)

    f32 = jnp.float32
    full = a_ref[...].astype(f32) + ar_ref[...].astype(f32)
    other = b_ref[...].astype(f32) + br_ref[...].astype(f32)
    slot = lax.broadcasted_iota(jnp.int32, full.shape, 0)
    products = jnp.where(slot < len_ref[seq], full * other, 0.0)
    acc[pl.ds(seq, 1), :] = jnp.sum(products, axis=0, keepdims=True)

    @pl.when(i == count - 1)
    def _():
        columns = acc.shape[1]
        c = lax.broadcasted_iota(jnp.int32, (columns, LANES), 0)
        lane = lax.broadcasted_iota(jnp.int32, (columns, LANES), 1)
        pick = jnp.where(c // R == lane % Q, 1.0, 0.0).astype(f32)
        spread = jnp.dot(acc[...], pick, precision=lax.Precision.HIGHEST, preferred_element_type=f32)
        row = lax.broadcasted_iota(jnp.int32, spread.shape, 0)
        place = lax.broadcasted_iota(jnp.int32, spread.shape, 1) // Q
        flat = jnp.sum(jnp.where(row == place, spread, 0.0), axis=0, keepdims=True)
        o_ref[...] = jnp.broadcast_to(flat, o_ref.shape)


def partial_scores(side, lengths, a, ar, b, br, devices):
    half, columns = a.shape
    seq_dev = lengths.shape[0]
    count = seq_dev // 2
    tile = half // count
    spec = pl.BlockSpec((tile, columns), lambda i, side, lens: (i, 0))
    return pl.pallas_call(
        functools.partial(score_kernel, seq_dev, devices),
        grid_spec=pltpu.PrefetchScalarGridSpec(
            num_scalar_prefetch=2,
            grid=(count,),
            in_specs=[spec] * 4,
            out_specs=pl.BlockSpec((devices, LANES), lambda i, side, lens: (0, 0)),
            scratch_shapes=[pltpu.VMEM((seq_dev, columns), jnp.float32)],
        ),
        out_shape=jax.ShapeDtypeStruct((devices, LANES), jnp.float32),
        compiler_params=pltpu.CompilerParams(vmem_limit_bytes=16 << 20),
    )(side, lengths, a, ar, b, br)


def select_kernel(group, seq_dev, order_ref, x_ref, o_ref):
    for i in range(o_ref.shape[0]):
        r = order_ref[i]
        g = r // seq_dev
        s = r % seq_dev
        row = x_ref[pl.ds(g * group, 1), :]
        for k in range(1, group):
            row = row + x_ref[pl.ds(g * group + k, 1), :]
        row = pltpu.roll(row, (LANES - s * Q) % LANES, 1)
        o_ref[pl.ds(i, 1), :] = row[:, :Q]


def select_rows(row_order, gathered, group):
    seq_dev = row_order.shape[0]
    return pl.pallas_call(
        functools.partial(select_kernel, group, seq_dev),
        in_specs=[pl.BlockSpec(memory_space=pltpu.SMEM), pl.BlockSpec(memory_space=pltpu.VMEM)],
        out_specs=pl.BlockSpec(memory_space=pltpu.VMEM),
        out_shape=jax.ShapeDtypeStruct((seq_dev, Q), jnp.float32),
        compiler_params=pltpu.CompilerParams(vmem_limit_bytes=8 << 20),
    )(row_order, gathered)


def square_on_device(n_seq, layer_inputs, out_grads, lengths, row_order, query_in, query_out):
    group = 4
    devices = n_seq * group
    seq_dev, seq_len, width_in = layer_inputs.shape
    flat_in = layer_inputs.reshape(seq_dev * seq_len, width_in)
    flat_out = out_grads.reshape(seq_dev * seq_len, out_grads.shape[2])
    axes = ("seq", "feat")
    first = [(s * group + f, s * group + (f ^ (1 if s % 2 == 0 else 2))) for s in range(n_seq) for f in range(group)]
    second = [(s * group + f, s * group + (f ^ (2 if s % 2 == 0 else 1))) for s in range(n_seq) for f in range(group)]
    feat = lax.axis_index("feat")
    odd = lax.axis_index("seq") % 2
    side = ((feat >> odd) & 1).astype(jnp.int32)
    keep, give = side[None], (1 - side)[None]

    a_give = half_matmul(flat_in, query_in, give, 512)
    a_got = lax.ppermute(a_give, axes, first)
    a_keep = half_matmul(flat_in, query_in, keep, 512)
    b_give = half_matmul(flat_out, query_out, give, 256)
    b_got = lax.ppermute(b_give, axes, first)
    a_pair = (a_keep.astype(jnp.float32) + a_got.astype(jnp.float32)).astype(jnp.bfloat16)
    a_far = lax.ppermute(a_pair, axes, second)
    b_keep = half_matmul(flat_out, query_out, keep, 256)
    mine = partial_scores(keep, lengths, a_pair, a_far, b_keep, b_got, devices)
    gathered = lax.all_to_all(mine, axes, 0, 0, tiled=True)
    return select_rows(row_order, gathered, group)


def on_device(layer_inputs, out_grads, lengths, row_order, query_in, query_out):
    seq_dev, seq_len, width_in = layer_inputs.shape
    total_rows = seq_dev * seq_len
    columns = query_in.shape[1]
    flat_in = layer_inputs.reshape(total_rows, width_in)
    flat_out = out_grads.reshape(total_rows, out_grads.shape[2])
    projected = lax.psum_scatter(
        jnp.concatenate(
            [
                jnp.dot(flat_in, query_in, preferred_element_type=jnp.float32),
                jnp.dot(flat_out, query_out, preferred_element_type=jnp.float32),
            ],
            axis=1,
        ).astype(jnp.bfloat16),
        "feat",
        scatter_dimension=0,
        tiled=True,
    ).astype(jnp.float32)
    first_row = lax.axis_index("feat") * projected.shape[0]
    row_count = projected.shape[0]
    products = projected[:, :columns] * projected[:, columns:]
    row_index = first_row + jnp.arange(row_count, dtype=jnp.int32)
    seq_owner = row_index // seq_len
    position = row_index % seq_len
    membership = (seq_owner[None, :] == jnp.arange(seq_dev, dtype=jnp.int32)[:, None]) & (
        position[None, :] < lengths[:, None]
    )
    seq_sums = jnp.dot(membership.astype(jnp.float32), products, precision=lax.Precision.HIGHEST)
    local_scores = seq_sums.reshape(seq_dev, Q, R).sum(axis=2)
    all_seqs = seq_dev * lax.axis_size("seq")
    placed = lax.dynamic_update_slice_in_dim(
        jnp.zeros((all_seqs, Q), jnp.float32), local_scores, lax.axis_index("seq") * seq_dev, 0
    )
    gathered = lax.psum(placed, ("seq", "feat"))
    selector = (row_order[:, None] == jnp.arange(all_seqs, dtype=jnp.int32)[None, :]).astype(
        jnp.float32
    )
    return jnp.dot(selector, gathered, precision=lax.Precision.HIGHEST)


def solution(mesh):
    n_seq, n_feat = mesh.shape["seq"], mesh.shape["feat"]
    body = functools.partial(square_on_device, n_seq) if n_feat == 4 and n_seq % 2 == 0 else on_device
    return jax.shard_map(
        body,
        mesh=mesh,
        in_specs=(
            P("seq", None, "feat"),
            P("seq", None, "feat"),
            P("seq"),
            P("seq"),
            P("feat", None),
            P("feat", None),
        ),
        out_specs=P("seq", None),
        check_vma=False,
    )
```

```python
import functools

import jax
import jax.numpy as jnp
from jax import lax
from jax.experimental import pallas as pl
from jax.experimental.pallas import tpu as pltpu
from jax.sharding import PartitionSpec as P

Q = 16
R = 32
LANES = 128
SIXTEENTHS = (10, 11, 12, 13, 14, 16)


GRAIN = 16
PIECE = 128


def fetch(side_ref, len_ref, x_ref, rows, table, counts, sems, half, tile):
    chunks = half // tile
    seq_dev = len_ref.shape[0]
    seq_len = x_ref.shape[0] // seq_dev
    first = side_ref[0] * (half // GRAIN)
    last = first + half // GRAIN
    for c in range(chunks):
        counts[c] = 0

    def one_seq(s, before):
        grains = (len_ref[s] + GRAIN - 1) // GRAIN
        low = jnp.maximum(before, first)
        high = jnp.minimum(before + grains, last)

        @pl.when(high > low)
        def _():
            start = (low - before) // (PIECE // GRAIN)
            stop = (high - before + PIECE // GRAIN - 1) // (PIECE // GRAIN)

            @pl.loop(start, stop)
            def _(p):
                place = pl.ds(pl.multiple_of(s * seq_len + p * PIECE, PIECE), PIECE)
                target = (jnp.maximum(before + p * (PIECE // GRAIN), low) - first) * GRAIN
                chunk = sum((target >= c * tile).astype(jnp.int32) for c in range(1, chunks)) if chunks > 1 else 0
                counts[chunk] = counts[chunk] + 1
                pltpu.make_async_copy(x_ref.at[place, :], rows.at[place, :], sems.at[chunk]).start()

            @pl.loop(low, high)
            def _(g):
                table[g - first] = s * seq_len + (g - before) * GRAIN

        return before + grains

    packed = lax.fori_loop(0, seq_dev, one_seq, 0)

    @pl.loop(jnp.maximum(packed, first), last)
    def _(g):
        table[g - first] = 0


def multiply(x_ref, rows, w_ref, o_ref, table, counts, sems, half, tile):
    @pl.loop(0, half // tile)
    def _(c):
        @pl.loop(0, counts[c])
        def _(i):
            place = pl.ds(0, PIECE)
            pltpu.make_async_copy(x_ref.at[place, :], rows.at[place, :], sems.at[c]).wait()

        left = jnp.concatenate(
            [
                rows[pl.ds(pl.multiple_of(table[c * (tile // GRAIN) + j], GRAIN), GRAIN), :]
                for j in range(tile // GRAIN)
            ],
            axis=0,
        )
        here = pl.ds(pl.multiple_of(c * tile, tile), tile)
        o_ref[here, :] = jnp.dot(left, w_ref[...], preferred_element_type=jnp.float32).astype(o_ref.dtype)


def scratch_for(x, half, tile):
    return [
        pltpu.VMEM(x.shape, x.dtype),
        pltpu.SMEM((half // GRAIN,), jnp.int32),
        pltpu.SMEM((half // tile,), jnp.int32),
        pltpu.SemaphoreType.DMA((half // tile,)),
    ]


def tile_of(half, limit):
    return max(t for t in range(GRAIN, limit + 1, GRAIN) if half % t == 0)


def cost(half, *pairs):
    return pl.CostEstimate(
        flops=sum(2 * half * w.shape[0] * w.shape[1] for _, w in pairs),
        bytes_accessed=sum(2 * half * (w.shape[0] + w.shape[1]) for _, w in pairs),
        transcendentals=0,
    )


SMEM_SPEC = pl.BlockSpec(memory_space=pltpu.SMEM)
HBM_SPEC = pl.BlockSpec(memory_space=pltpu.HBM)
VMEM_SPEC = pl.BlockSpec(memory_space=pltpu.VMEM)


def own_weights_kernel(half, tile, side_ref, len_ref, x_ref, w_hbm, o_ref, w_ref, w_sem, *work):
    copy = pltpu.make_async_copy(w_hbm, w_ref, w_sem)
    copy.start()
    fetch(side_ref, len_ref, x_ref, *work, half, tile)
    copy.wait()
    multiply(x_ref, work[0], w_ref, o_ref, *work[1:], half, tile)


def own_weights_matmul(side, lengths, x, w, half):
    tile = tile_of(half, 384)
    return pl.pallas_call(
        functools.partial(own_weights_kernel, half, tile),
        in_specs=[SMEM_SPEC, SMEM_SPEC, HBM_SPEC, HBM_SPEC],
        out_specs=VMEM_SPEC,
        out_shape=jax.ShapeDtypeStruct((half, w.shape[1]), jnp.bfloat16),
        scratch_shapes=[pltpu.VMEM(w.shape, w.dtype), pltpu.SemaphoreType.DMA] + scratch_for(x, half, tile),
        compiler_params=pltpu.CompilerParams(vmem_limit_bytes=16 << 20),
        cost_estimate=cost(half, (x, w)),
    )(side, lengths, x, w)


def half_kernel(half, tile, side_ref, len_ref, x_ref, w_ref, o_ref, *work):
    fetch(side_ref, len_ref, x_ref, *work, half, tile)
    multiply(x_ref, work[0], w_ref, o_ref, *work[1:], half, tile)


def half_matmul(side, lengths, x, w, half):
    tile = tile_of(half, 352)
    return pl.pallas_call(
        functools.partial(half_kernel, half, tile),
        in_specs=[SMEM_SPEC, SMEM_SPEC, HBM_SPEC, VMEM_SPEC],
        out_specs=VMEM_SPEC,
        out_shape=jax.ShapeDtypeStruct((half, w.shape[1]), jnp.bfloat16),
        scratch_shapes=scratch_for(x, half, tile),
        compiler_params=pltpu.CompilerParams(vmem_limit_bytes=36 << 20),
        cost_estimate=cost(half, (x, w)),
    )(side, lengths, x, w)


def score_kernel(tile, side_ref, len_ref, a_ref, ar_ref, b_ref, br_ref, o_ref):
    f32, bf16 = jnp.float32, jnp.bfloat16
    half, columns = a_ref.shape
    seq_dev = len_ref.shape[0]
    base = side_ref[0] * half
    seq = lax.broadcasted_iota(jnp.int32, (seq_dev, 1), 0)
    opens = jnp.zeros((seq_dev, 1), jnp.int32)
    closes = jnp.zeros((seq_dev, 1), jnp.int32)
    used = -base
    for s in range(seq_dev):
        opens = jnp.where(seq == s, used, opens)
        closes = jnp.where(seq == s, used + len_ref[s], closes)
        used = used + (len_ref[s] + GRAIN - 1) // GRAIN * GRAIN
    sums = jnp.zeros((seq_dev, columns), f32)
    for c in range(half // tile):
        here = pl.ds(c * tile, tile)
        full = a_ref[here, :].astype(f32) + ar_ref[here, :].astype(f32)
        other = b_ref[here, :].astype(f32) + br_ref[here, :].astype(f32)
        slot = lax.broadcasted_iota(jnp.int32, (tile, columns), 0) + c * tile
        products = jnp.where(slot < used, full * other, 0.0)
        place = lax.broadcasted_iota(jnp.int32, (seq_dev, tile), 1) + c * tile
        member = jnp.where((place >= opens) & (place < closes), 1.0, 0.0).astype(bf16)
        high = products.astype(bf16)
        rest = products - high.astype(f32)
        middle = rest.astype(bf16)
        low = (rest - middle.astype(f32)).astype(bf16)
        for part in (high, middle, low):
            sums = sums + jnp.dot(member, part, preferred_element_type=f32)
    c = lax.broadcasted_iota(jnp.int32, (columns, LANES), 0)
    lane = lax.broadcasted_iota(jnp.int32, (columns, LANES), 1)
    pick = jnp.where(c // R == lane % Q, 1.0, 0.0).astype(f32)
    spread = jnp.dot(sums, pick, precision=lax.Precision.HIGHEST, preferred_element_type=f32)
    row = lax.broadcasted_iota(jnp.int32, spread.shape, 0)
    place = lax.broadcasted_iota(jnp.int32, spread.shape, 1) // Q
    flat = jnp.sum(jnp.where(row == place, spread, 0.0), axis=0, keepdims=True)
    o_ref[...] = jnp.broadcast_to(flat, o_ref.shape)


def partial_scores(side, lengths, a, ar, b, br, devices, tile):
    return pl.pallas_call(
        functools.partial(score_kernel, tile),
        in_specs=[pl.BlockSpec(memory_space=pltpu.SMEM)] * 2 + [pl.BlockSpec(memory_space=pltpu.VMEM)] * 4,
        out_specs=pl.BlockSpec(memory_space=pltpu.VMEM),
        out_shape=jax.ShapeDtypeStruct((devices, LANES), jnp.float32),
        compiler_params=pltpu.CompilerParams(vmem_limit_bytes=16 << 20),
    )(side, lengths, a, ar, b, br)


def select_kernel(group, seq_dev, order_ref, x_ref, o_ref):
    for i in range(o_ref.shape[0]):
        r = order_ref[i]
        g = r // seq_dev
        s = r % seq_dev
        row = x_ref[pl.ds(g * group, 1), :]
        for k in range(1, group):
            row = row + x_ref[pl.ds(g * group + k, 1), :]
        row = pltpu.roll(row, (LANES - s * Q) % LANES, 1)
        o_ref[pl.ds(i, 1), :] = row[:, :Q]


def select_rows(row_order, gathered, group):
    seq_dev = row_order.shape[0]
    return pl.pallas_call(
        functools.partial(select_kernel, group, seq_dev),
        in_specs=[pl.BlockSpec(memory_space=pltpu.SMEM), pl.BlockSpec(memory_space=pltpu.VMEM)],
        out_specs=pl.BlockSpec(memory_space=pltpu.VMEM),
        out_shape=jax.ShapeDtypeStruct((seq_dev, Q), jnp.float32),
        compiler_params=pltpu.CompilerParams(vmem_limit_bytes=8 << 20),
    )(row_order, gathered)


def square_on_device(n_seq, layer_inputs, out_grads, lengths, row_order, query_in, query_out):
    group = 4
    devices = n_seq * group
    seq_dev, seq_len, width_in = layer_inputs.shape
    flat_in = layer_inputs.reshape(seq_dev * seq_len, width_in)
    flat_out = out_grads.reshape(seq_dev * seq_len, out_grads.shape[2])
    axes = ("seq", "feat")
    first = [(s * group + f, s * group + (f ^ (1 if s % 2 == 0 else 2))) for s in range(n_seq) for f in range(group)]
    second = [(s * group + f, s * group + (f ^ (2 if s % 2 == 0 else 1))) for s in range(n_seq) for f in range(group)]
    feat = lax.axis_index("feat")
    odd = lax.axis_index("seq") % 2
    side = ((feat >> odd) & 1).astype(jnp.int32)
    keep, give = side[None], (1 - side)[None]

    def sized(half):
        def run():
            a_give = own_weights_matmul(give, lengths, flat_in, query_in, half)
            a_give, weights_out = lax.optimization_barrier((a_give, query_out))
            a_got = lax.ppermute(a_give, axes, first)
            b_give = half_matmul(give, lengths, flat_out, weights_out, half)
            b_got = lax.ppermute(b_give, axes, first)
            a_keep = own_weights_matmul(keep, lengths, flat_in, query_in, half)
            a_pair = (a_keep.astype(jnp.float32) + a_got.astype(jnp.float32)).astype(jnp.bfloat16)
            a_far = lax.ppermute(a_pair, axes, second)
            b_keep = half_matmul(keep, lengths, flat_out, weights_out, half)
            return partial_scores(keep, lengths, a_pair, a_far, b_keep, b_got, devices, tile_of(half, 384))

        return run

    total = seq_dev * seq_len
    halves = [total * k // 32 for k in SIXTEENTHS]
    packed = jnp.sum((lengths + GRAIN - 1) // GRAIN) * GRAIN
    which = sum((packed > 2 * half).astype(jnp.int32) for half in halves[:-1])
    mine = lax.switch(which, [sized(half) for half in halves])
    gathered = lax.all_to_all(mine, axes, 0, 0, tiled=True)
    return select_rows(row_order, gathered, group)


def on_device(layer_inputs, out_grads, lengths, row_order, query_in, query_out):
    seq_dev, seq_len, width_in = layer_inputs.shape
    total_rows = seq_dev * seq_len
    columns = query_in.shape[1]
    flat_in = layer_inputs.reshape(total_rows, width_in)
    flat_out = out_grads.reshape(total_rows, out_grads.shape[2])
    projected = lax.psum_scatter(
        jnp.concatenate(
            [
                jnp.dot(flat_in, query_in, preferred_element_type=jnp.float32),
                jnp.dot(flat_out, query_out, preferred_element_type=jnp.float32),
            ],
            axis=1,
        ).astype(jnp.bfloat16),
        "feat",
        scatter_dimension=0,
        tiled=True,
    ).astype(jnp.float32)
    first_row = lax.axis_index("feat") * projected.shape[0]
    row_count = projected.shape[0]
    products = projected[:, :columns] * projected[:, columns:]
    row_index = first_row + jnp.arange(row_count, dtype=jnp.int32)
    seq_owner = row_index // seq_len
    position = row_index % seq_len
    membership = (seq_owner[None, :] == jnp.arange(seq_dev, dtype=jnp.int32)[:, None]) & (
        position[None, :] < lengths[:, None]
    )
    seq_sums = jnp.dot(membership.astype(jnp.float32), products, precision=lax.Precision.HIGHEST)
    local_scores = seq_sums.reshape(seq_dev, Q, R).sum(axis=2)
    all_seqs = seq_dev * lax.axis_size("seq")
    placed = lax.dynamic_update_slice_in_dim(
        jnp.zeros((all_seqs, Q), jnp.float32), local_scores, lax.axis_index("seq") * seq_dev, 0
    )
    gathered = lax.psum(placed, ("seq", "feat"))
    selector = (row_order[:, None] == jnp.arange(all_seqs, dtype=jnp.int32)[None, :]).astype(
        jnp.float32
    )
    return jnp.dot(selector, gathered, precision=lax.Precision.HIGHEST)


def solution(mesh):
    n_seq, n_feat = mesh.shape["seq"], mesh.shape["feat"]
    body = functools.partial(square_on_device, n_seq) if n_feat == 4 and n_seq % 2 == 0 else on_device
    return jax.shard_map(
        body,
        mesh=mesh,
        in_specs=(
            P("seq", None, "feat"),
            P("seq", None, "feat"),
            P("seq"),
            P("seq"),
            P("feat", None),
            P("feat", None),
        ),
        out_specs=P("seq", None),
        check_vma=False,
    )
```

```python
import functools

import jax
import jax.numpy as jnp
from jax import lax
from jax.experimental import pallas as pl
from jax.experimental.pallas import tpu as pltpu
from jax.sharding import PartitionSpec as P

Q = 16
R = 32
LANES = 128
SIXTEENTHS = (11, 12, 13, 14, 15, 16)


GRAIN = 16
PIECE = 64


def fetch(side_ref, len_ref, x_ref, rows, table, counts, sems, half, tile):
    chunks = half // tile
    seq_dev = len_ref.shape[0]
    seq_len = x_ref.shape[0] // seq_dev
    first = side_ref[0] * (half // GRAIN)
    last = first + half // GRAIN
    for c in range(chunks):
        counts[c] = 0

    def one_seq(s, before):
        grains = (len_ref[s] + GRAIN - 1) // GRAIN
        low = jnp.maximum(before, first)
        high = jnp.minimum(before + grains, last)

        @pl.when(high > low)
        def _():
            start = (low - before) // (PIECE // GRAIN)
            stop = (high - before + PIECE // GRAIN - 1) // (PIECE // GRAIN)

            @pl.loop(start, stop)
            def _(p):
                place = pl.ds(pl.multiple_of(s * seq_len + p * PIECE, PIECE), PIECE)
                target = (jnp.maximum(before + p * (PIECE // GRAIN), low) - first) * GRAIN
                chunk = sum((target >= c * tile).astype(jnp.int32) for c in range(1, chunks)) if chunks > 1 else 0
                counts[chunk] = counts[chunk] + 1
                pltpu.make_async_copy(x_ref.at[place, :], rows.at[place, :], sems.at[chunk]).start()

            @pl.loop(low, high)
            def _(g):
                table[g - first] = s * seq_len + (g - before) * GRAIN

        return before + grains

    packed = lax.fori_loop(0, seq_dev, one_seq, 0)

    @pl.loop(jnp.maximum(packed, first), last)
    def _(g):
        table[g - first] = 0


def multiply(x_ref, rows, w_ref, o_ref, table, counts, sems, half, tile):
    @pl.loop(0, half // tile)
    def _(c):
        @pl.loop(0, counts[c])
        def _(i):
            place = pl.ds(0, PIECE)
            pltpu.make_async_copy(x_ref.at[place, :], rows.at[place, :], sems.at[c]).wait()

        left = jnp.concatenate(
            [
                rows[pl.ds(pl.multiple_of(table[c * (tile // GRAIN) + j], GRAIN), GRAIN), :]
                for j in range(tile // GRAIN)
            ],
            axis=0,
        )
        here = pl.ds(pl.multiple_of(c * tile, tile), tile)
        o_ref[here, :] = jnp.dot(left, w_ref[...], preferred_element_type=jnp.float32).astype(o_ref.dtype)


def scratch_for(x, half, tile):
    return [
        pltpu.VMEM(x.shape, x.dtype),
        pltpu.SMEM((half // GRAIN,), jnp.int32),
        pltpu.SMEM((half // tile,), jnp.int32),
        pltpu.SemaphoreType.DMA((half // tile,)),
    ]


def tile_of(half, limit):
    return max(t for t in range(GRAIN, limit + 1, GRAIN) if half % t == 0)


def cost(half, *pairs):
    return pl.CostEstimate(
        flops=sum(2 * half * w.shape[0] * w.shape[1] for _, w in pairs),
        bytes_accessed=sum(2 * half * (w.shape[0] + w.shape[1]) for _, w in pairs),
        transcendentals=0,
    )


SMEM_SPEC = pl.BlockSpec(memory_space=pltpu.SMEM)
HBM_SPEC = pl.BlockSpec(memory_space=pltpu.HBM)
VMEM_SPEC = pl.BlockSpec(memory_space=pltpu.VMEM)


def own_weights_kernel(half, tile, side_ref, len_ref, x_ref, w_hbm, o_ref, w_ref, w_sem, *work):
    copy = pltpu.make_async_copy(w_hbm, w_ref, w_sem)
    copy.start()
    fetch(side_ref, len_ref, x_ref, *work, half, tile)
    copy.wait()
    multiply(x_ref, work[0], w_ref, o_ref, *work[1:], half, tile)


def own_weights_matmul(side, lengths, x, w, half):
    tile = tile_of(half, 384)
    return pl.pallas_call(
        functools.partial(own_weights_kernel, half, tile),
        in_specs=[SMEM_SPEC, SMEM_SPEC, HBM_SPEC, HBM_SPEC],
        out_specs=VMEM_SPEC,
        out_shape=jax.ShapeDtypeStruct((half, w.shape[1]), jnp.bfloat16),
        scratch_shapes=[pltpu.VMEM(w.shape, w.dtype), pltpu.SemaphoreType.DMA] + scratch_for(x, half, tile),
        compiler_params=pltpu.CompilerParams(vmem_limit_bytes=16 << 20),
        cost_estimate=cost(half, (x, w)),
    )(side, lengths, x, w)


def half_kernel(half, tile, side_ref, len_ref, x_ref, w_ref, o_ref, *work):
    fetch(side_ref, len_ref, x_ref, *work, half, tile)
    multiply(x_ref, work[0], w_ref, o_ref, *work[1:], half, tile)


def half_matmul(side, lengths, x, w, half, limit=352, grant=36):
    tile = tile_of(half, limit)
    return pl.pallas_call(
        functools.partial(half_kernel, half, tile),
        in_specs=[SMEM_SPEC, SMEM_SPEC, HBM_SPEC, VMEM_SPEC],
        out_specs=VMEM_SPEC,
        out_shape=jax.ShapeDtypeStruct((half, w.shape[1]), jnp.bfloat16),
        scratch_shapes=scratch_for(x, half, tile),
        compiler_params=pltpu.CompilerParams(vmem_limit_bytes=grant << 20),
        cost_estimate=cost(half, (x, w)),
    )(side, lengths, x, w)


def score_kernel(tile, side_ref, len_ref, a_ref, ar_ref, b_ref, br_ref, o_ref):
    f32, bf16 = jnp.float32, jnp.bfloat16
    half, columns = a_ref.shape
    seq_dev = len_ref.shape[0]
    base = side_ref[0] * half
    seq = lax.broadcasted_iota(jnp.int32, (seq_dev, 1), 0)
    opens = jnp.zeros((seq_dev, 1), jnp.int32)
    closes = jnp.zeros((seq_dev, 1), jnp.int32)
    used = -base
    for s in range(seq_dev):
        opens = jnp.where(seq == s, used, opens)
        closes = jnp.where(seq == s, used + len_ref[s], closes)
        used = used + (len_ref[s] + GRAIN - 1) // GRAIN * GRAIN
    sums = jnp.zeros((seq_dev, columns), f32)
    for c in range(half // tile):
        here = pl.ds(c * tile, tile)
        full = a_ref[here, :].astype(f32) + ar_ref[here, :].astype(f32)
        other = b_ref[here, :].astype(f32) + br_ref[here, :].astype(f32)
        slot = lax.broadcasted_iota(jnp.int32, (tile, columns), 0) + c * tile
        products = jnp.where(slot < used, full * other, 0.0)
        place = lax.broadcasted_iota(jnp.int32, (seq_dev, tile), 1) + c * tile
        member = jnp.where((place >= opens) & (place < closes), 1.0, 0.0).astype(bf16)
        high = products.astype(bf16)
        low = (products - high.astype(f32)).astype(bf16)
        for part in (high, low):
            sums = sums + jnp.dot(member, part, preferred_element_type=f32)
    c = lax.broadcasted_iota(jnp.int32, (columns, LANES), 0)
    lane = lax.broadcasted_iota(jnp.int32, (columns, LANES), 1)
    pick = jnp.where(c // R == lane % Q, 1.0, 0.0).astype(f32)
    spread = jnp.dot(sums, pick, precision=lax.Precision.HIGHEST, preferred_element_type=f32)
    row = lax.broadcasted_iota(jnp.int32, spread.shape, 0)
    place = lax.broadcasted_iota(jnp.int32, spread.shape, 1) // Q
    flat = jnp.sum(jnp.where(row == place, spread, 0.0), axis=0, keepdims=True)
    o_ref[...] = jnp.broadcast_to(flat, o_ref.shape)


def partial_scores(side, lengths, a, ar, b, br, devices, tile):
    return pl.pallas_call(
        functools.partial(score_kernel, tile),
        in_specs=[pl.BlockSpec(memory_space=pltpu.SMEM)] * 2 + [pl.BlockSpec(memory_space=pltpu.VMEM)] * 4,
        out_specs=pl.BlockSpec(memory_space=pltpu.VMEM),
        out_shape=jax.ShapeDtypeStruct((devices, LANES), jnp.float32),
        compiler_params=pltpu.CompilerParams(vmem_limit_bytes=16 << 20),
    )(side, lengths, a, ar, b, br)


def select_kernel(group, seq_dev, order_ref, x_ref, o_ref):
    for i in range(o_ref.shape[0]):
        r = order_ref[i]
        g = r // seq_dev
        s = r % seq_dev
        row = x_ref[pl.ds(g * group, 1), :]
        for k in range(1, group):
            row = row + x_ref[pl.ds(g * group + k, 1), :]
        row = pltpu.roll(row, (LANES - s * Q) % LANES, 1)
        o_ref[pl.ds(i, 1), :] = row[:, :Q]


def select_rows(row_order, gathered, group):
    seq_dev = row_order.shape[0]
    return pl.pallas_call(
        functools.partial(select_kernel, group, seq_dev),
        in_specs=[pl.BlockSpec(memory_space=pltpu.SMEM), pl.BlockSpec(memory_space=pltpu.VMEM)],
        out_specs=pl.BlockSpec(memory_space=pltpu.VMEM),
        out_shape=jax.ShapeDtypeStruct((seq_dev, Q), jnp.float32),
        compiler_params=pltpu.CompilerParams(vmem_limit_bytes=8 << 20),
    )(row_order, gathered)


def square_on_device(n_seq, layer_inputs, out_grads, lengths, row_order, query_in, query_out):
    group = 4
    devices = n_seq * group
    seq_dev, seq_len, width_in = layer_inputs.shape
    flat_in = layer_inputs.reshape(seq_dev * seq_len, width_in)
    flat_out = out_grads.reshape(seq_dev * seq_len, out_grads.shape[2])
    axes = ("seq", "feat")
    first = [(s * group + f, s * group + (f ^ (1 if s % 2 == 0 else 2))) for s in range(n_seq) for f in range(group)]
    second = [(s * group + f, s * group + (f ^ (2 if s % 2 == 0 else 1))) for s in range(n_seq) for f in range(group)]
    feat = lax.axis_index("feat")
    odd = lax.axis_index("seq") % 2
    side = ((feat >> odd) & 1).astype(jnp.int32)
    keep, give = side[None], (1 - side)[None]

    def sized(half):
        def run():
            a_give = own_weights_matmul(give, lengths, flat_in, query_in, half)
            a_got = lax.ppermute(a_give, axes, first)
            b_give = half_matmul(give, lengths, flat_out, query_out, half)
            b_got = lax.ppermute(b_give, axes, first)
            a_keep = half_matmul(keep, lengths, flat_in, query_in, half, 384, 14)
            a_pair = (a_keep.astype(jnp.float32) + a_got.astype(jnp.float32)).astype(jnp.bfloat16)
            a_far = lax.ppermute(a_pair, axes, second)
            b_keep = half_matmul(keep, lengths, flat_out, query_out, half)
            return partial_scores(keep, lengths, a_pair, a_far, b_keep, b_got, devices, tile_of(half, 384))

        return run

    total = seq_dev * seq_len
    halves = [total * k // 32 for k in SIXTEENTHS]
    packed = jnp.sum((lengths + GRAIN - 1) // GRAIN) * GRAIN
    which = sum((packed > 2 * half).astype(jnp.int32) for half in halves[:-1])
    mine = lax.switch(which, [sized(half) for half in halves])
    gathered = lax.all_to_all(mine, axes, 0, 0, tiled=True)
    return select_rows(row_order, gathered, group)


def on_device(layer_inputs, out_grads, lengths, row_order, query_in, query_out):
    seq_dev, seq_len, width_in = layer_inputs.shape
    total_rows = seq_dev * seq_len
    columns = query_in.shape[1]
    flat_in = layer_inputs.reshape(total_rows, width_in)
    flat_out = out_grads.reshape(total_rows, out_grads.shape[2])
    projected = lax.psum_scatter(
        jnp.concatenate(
            [
                jnp.dot(flat_in, query_in, preferred_element_type=jnp.float32),
                jnp.dot(flat_out, query_out, preferred_element_type=jnp.float32),
            ],
            axis=1,
        ).astype(jnp.bfloat16),
        "feat",
        scatter_dimension=0,
        tiled=True,
    ).astype(jnp.float32)
    first_row = lax.axis_index("feat") * projected.shape[0]
    row_count = projected.shape[0]
    products = projected[:, :columns] * projected[:, columns:]
    row_index = first_row + jnp.arange(row_count, dtype=jnp.int32)
    seq_owner = row_index // seq_len
    position = row_index % seq_len
    membership = (seq_owner[None, :] == jnp.arange(seq_dev, dtype=jnp.int32)[:, None]) & (
        position[None, :] < lengths[:, None]
    )
    seq_sums = jnp.dot(membership.astype(jnp.float32), products, precision=lax.Precision.HIGHEST)
    local_scores = seq_sums.reshape(seq_dev, Q, R).sum(axis=2)
    all_seqs = seq_dev * lax.axis_size("seq")
    placed = lax.dynamic_update_slice_in_dim(
        jnp.zeros((all_seqs, Q), jnp.float32), local_scores, lax.axis_index("seq") * seq_dev, 0
    )
    gathered = lax.psum(placed, ("seq", "feat"))
    selector = (row_order[:, None] == jnp.arange(all_seqs, dtype=jnp.int32)[None, :]).astype(
        jnp.float32
    )
    return jnp.dot(selector, gathered, precision=lax.Precision.HIGHEST)


def solution(mesh):
    n_seq, n_feat = mesh.shape["seq"], mesh.shape["feat"]
    body = functools.partial(square_on_device, n_seq) if n_feat == 4 and n_seq % 2 == 0 else on_device
    return jax.shard_map(
        body,
        mesh=mesh,
        in_specs=(
            P("seq", None, "feat"),
            P("seq", None, "feat"),
            P("seq"),
            P("seq"),
            P("feat", None),
            P("feat", None),
        ),
        out_specs=P("seq", None),
        check_vma=False,
    )
```

```python
import functools

import jax
import jax.numpy as jnp
from jax import lax
from jax.experimental import pallas as pl
from jax.experimental.pallas import tpu as pltpu
from jax.sharding import PartitionSpec as P

Q = 16
R = 32
LANES = 128
SIXTEENTHS = (11, 12, 13, 14, 15, 16)


GRAIN = 16
PIECE = 64


def fetch(side_ref, len_ref, x_ref, rows, table, counts, sems, half, tile):
    chunks = half // tile
    seq_dev = len_ref.shape[0]
    seq_len = x_ref.shape[0] // seq_dev
    first = side_ref[0] * (half // GRAIN)
    last = first + half // GRAIN
    for c in range(chunks):
        counts[c] = 0

    def one_seq(s, before):
        grains = (len_ref[s] + GRAIN - 1) // GRAIN
        low = jnp.maximum(before, first)
        high = jnp.minimum(before + grains, last)

        @pl.when(high > low)
        def _():
            start = (low - before) // (PIECE // GRAIN)
            stop = (high - before + PIECE // GRAIN - 1) // (PIECE // GRAIN)

            @pl.loop(start, stop)
            def _(p):
                place = pl.ds(pl.multiple_of(s * seq_len + p * PIECE, PIECE), PIECE)
                target = (jnp.maximum(before + p * (PIECE // GRAIN), low) - first) * GRAIN
                chunk = sum((target >= c * tile).astype(jnp.int32) for c in range(1, chunks)) if chunks > 1 else 0
                counts[chunk] = counts[chunk] + 1
                pltpu.make_async_copy(x_ref.at[place, :], rows.at[place, :], sems.at[chunk]).start()

            @pl.loop(low, high)
            def _(g):
                table[g - first] = s * seq_len + (g - before) * GRAIN

        return before + grains

    packed = lax.fori_loop(0, seq_dev, one_seq, 0)

    @pl.loop(jnp.maximum(packed, first), last)
    def _(g):
        table[g - first] = 0


def multiply(x_ref, rows, w_ref, o_ref, table, counts, sems, half, tile):
    @pl.loop(0, half // tile)
    def _(c):
        @pl.loop(0, counts[c])
        def _(i):
            place = pl.ds(0, PIECE)
            pltpu.make_async_copy(x_ref.at[place, :], rows.at[place, :], sems.at[c]).wait()

        left = jnp.concatenate(
            [
                rows[pl.ds(pl.multiple_of(table[c * (tile // GRAIN) + j], GRAIN), GRAIN), :]
                for j in range(tile // GRAIN)
            ],
            axis=0,
        )
        here = pl.ds(pl.multiple_of(c * tile, tile), tile)
        o_ref[here, :] = jnp.dot(left, w_ref[...], preferred_element_type=jnp.float32).astype(o_ref.dtype)


def scratch_for(x, half, tile):
    return [
        pltpu.VMEM(x.shape, x.dtype),
        pltpu.SMEM((half // GRAIN,), jnp.int32),
        pltpu.SMEM((half // tile,), jnp.int32),
        pltpu.SemaphoreType.DMA((half // tile,)),
    ]


def tile_of(half, limit):
    return max(t for t in range(GRAIN, limit + 1, GRAIN) if half % t == 0)


def cost(half, *pairs):
    return pl.CostEstimate(
        flops=sum(2 * half * w.shape[0] * w.shape[1] for _, w in pairs),
        bytes_accessed=sum(2 * half * (w.shape[0] + w.shape[1]) for _, w in pairs),
        transcendentals=0,
    )


SMEM_SPEC = pl.BlockSpec(memory_space=pltpu.SMEM)
HBM_SPEC = pl.BlockSpec(memory_space=pltpu.HBM)
VMEM_SPEC = pl.BlockSpec(memory_space=pltpu.VMEM)


def own_weights_kernel(half, tile, side_ref, len_ref, x_ref, w_hbm, o_ref, w_ref, w_sem, *work):
    copy = pltpu.make_async_copy(w_hbm, w_ref, w_sem)
    copy.start()
    fetch(side_ref, len_ref, x_ref, *work, half, tile)
    copy.wait()
    multiply(x_ref, work[0], w_ref, o_ref, *work[1:], half, tile)


def own_weights_matmul(side, lengths, x, w, half):
    tile = tile_of(half, 384)
    return pl.pallas_call(
        functools.partial(own_weights_kernel, half, tile),
        in_specs=[SMEM_SPEC, SMEM_SPEC, HBM_SPEC, HBM_SPEC],
        out_specs=VMEM_SPEC,
        out_shape=jax.ShapeDtypeStruct((half, w.shape[1]), jnp.bfloat16),
        scratch_shapes=[pltpu.VMEM(w.shape, w.dtype), pltpu.SemaphoreType.DMA] + scratch_for(x, half, tile),
        compiler_params=pltpu.CompilerParams(vmem_limit_bytes=16 << 20),
        cost_estimate=cost(half, (x, w)),
    )(side, lengths, x, w)


def resident_kernel(half, tile, side_ref, len_ref, x_ref, w_ref, o_ref, table):
    seq_dev = len_ref.shape[0]
    seq_len = x_ref.shape[0] // seq_dev
    first = side_ref[0] * (half // GRAIN)
    last = first + half // GRAIN

    def one_seq(s, before):
        after = before + (len_ref[s] + GRAIN - 1) // GRAIN

        @pl.loop(jnp.maximum(before, first), jnp.minimum(after, last))
        def _(g):
            table[g - first] = s * seq_len + (g - before) * GRAIN

        return after

    packed = lax.fori_loop(0, seq_dev, one_seq, 0)

    @pl.loop(jnp.maximum(packed, first), last)
    def _(g):
        table[g - first] = 0

    @pl.loop(0, half // tile)
    def _(c):
        left = jnp.concatenate(
            [
                x_ref[pl.ds(pl.multiple_of(table[c * (tile // GRAIN) + j], GRAIN), GRAIN), :]
                for j in range(tile // GRAIN)
            ],
            axis=0,
        )
        here = pl.ds(pl.multiple_of(c * tile, tile), tile)
        o_ref[here, :] = jnp.dot(left, w_ref[...], preferred_element_type=jnp.float32).astype(o_ref.dtype)


def resident_matmul(side, lengths, x, w, half):
    tile = tile_of(half, 384)
    return pl.pallas_call(
        functools.partial(resident_kernel, half, tile),
        in_specs=[SMEM_SPEC, SMEM_SPEC, VMEM_SPEC, VMEM_SPEC],
        out_specs=VMEM_SPEC,
        out_shape=jax.ShapeDtypeStruct((half, w.shape[1]), jnp.bfloat16),
        scratch_shapes=[pltpu.SMEM((half // GRAIN,), jnp.int32)],
        compiler_params=pltpu.CompilerParams(vmem_limit_bytes=14 << 20),
        cost_estimate=cost(half, (x, w)),
    )(side, lengths, x, w)


def half_kernel(half, tile, side_ref, len_ref, x_ref, w_ref, o_ref, *work):
    fetch(side_ref, len_ref, x_ref, *work, half, tile)
    multiply(x_ref, work[0], w_ref, o_ref, *work[1:], half, tile)


def half_matmul(side, lengths, x, w, half, limit=352, grant=36):
    tile = tile_of(half, limit)
    return pl.pallas_call(
        functools.partial(half_kernel, half, tile),
        in_specs=[SMEM_SPEC, SMEM_SPEC, HBM_SPEC, VMEM_SPEC],
        out_specs=VMEM_SPEC,
        out_shape=jax.ShapeDtypeStruct((half, w.shape[1]), jnp.bfloat16),
        scratch_shapes=scratch_for(x, half, tile),
        compiler_params=pltpu.CompilerParams(vmem_limit_bytes=grant << 20),
        cost_estimate=cost(half, (x, w)),
    )(side, lengths, x, w)


def score_kernel(tile, side_ref, len_ref, a_ref, ar_ref, b_ref, br_ref, o_ref):
    f32, bf16 = jnp.float32, jnp.bfloat16
    half, columns = a_ref.shape
    seq_dev = len_ref.shape[0]
    base = side_ref[0] * half
    seq = lax.broadcasted_iota(jnp.int32, (seq_dev, 1), 0)
    opens = jnp.zeros((seq_dev, 1), jnp.int32)
    closes = jnp.zeros((seq_dev, 1), jnp.int32)
    used = -base
    for s in range(seq_dev):
        opens = jnp.where(seq == s, used, opens)
        closes = jnp.where(seq == s, used + len_ref[s], closes)
        used = used + (len_ref[s] + GRAIN - 1) // GRAIN * GRAIN
    sums = jnp.zeros((seq_dev, columns), f32)
    for c in range(half // tile):
        here = pl.ds(c * tile, tile)
        full = a_ref[here, :].astype(f32) + ar_ref[here, :].astype(f32)
        other = b_ref[here, :].astype(f32) + br_ref[here, :].astype(f32)
        slot = lax.broadcasted_iota(jnp.int32, (tile, columns), 0) + c * tile
        products = jnp.where(slot < used, full * other, 0.0)
        place = lax.broadcasted_iota(jnp.int32, (seq_dev, tile), 1) + c * tile
        member = jnp.where((place >= opens) & (place < closes), 1.0, 0.0).astype(bf16)
        high = products.astype(bf16)
        low = (products - high.astype(f32)).astype(bf16)
        for part in (high, low):
            sums = sums + jnp.dot(member, part, preferred_element_type=f32)
    c = lax.broadcasted_iota(jnp.int32, (columns, LANES), 0)
    lane = lax.broadcasted_iota(jnp.int32, (columns, LANES), 1)
    pick = jnp.where(c // R == lane % Q, 1.0, 0.0).astype(f32)
    spread = jnp.dot(sums, pick, precision=lax.Precision.HIGHEST, preferred_element_type=f32)
    row = lax.broadcasted_iota(jnp.int32, spread.shape, 0)
    place = lax.broadcasted_iota(jnp.int32, spread.shape, 1) // Q
    flat = jnp.sum(jnp.where(row == place, spread, 0.0), axis=0, keepdims=True)
    o_ref[...] = jnp.broadcast_to(flat, o_ref.shape)


def partial_scores(side, lengths, a, ar, b, br, devices, tile):
    return pl.pallas_call(
        functools.partial(score_kernel, tile),
        in_specs=[pl.BlockSpec(memory_space=pltpu.SMEM)] * 2 + [pl.BlockSpec(memory_space=pltpu.VMEM)] * 4,
        out_specs=pl.BlockSpec(memory_space=pltpu.VMEM),
        out_shape=jax.ShapeDtypeStruct((devices, LANES), jnp.float32),
        compiler_params=pltpu.CompilerParams(vmem_limit_bytes=16 << 20),
    )(side, lengths, a, ar, b, br)


def select_kernel(group, seq_dev, order_ref, x_ref, o_ref):
    for i in range(o_ref.shape[0]):
        r = order_ref[i]
        g = r // seq_dev
        s = r % seq_dev
        row = x_ref[pl.ds(g * group, 1), :]
        for k in range(1, group):
            row = row + x_ref[pl.ds(g * group + k, 1), :]
        row = pltpu.roll(row, (LANES - s * Q) % LANES, 1)
        o_ref[pl.ds(i, 1), :] = row[:, :Q]


def select_rows(row_order, gathered, group):
    seq_dev = row_order.shape[0]
    return pl.pallas_call(
        functools.partial(select_kernel, group, seq_dev),
        in_specs=[pl.BlockSpec(memory_space=pltpu.SMEM), pl.BlockSpec(memory_space=pltpu.VMEM)],
        out_specs=pl.BlockSpec(memory_space=pltpu.VMEM),
        out_shape=jax.ShapeDtypeStruct((seq_dev, Q), jnp.float32),
        compiler_params=pltpu.CompilerParams(vmem_limit_bytes=8 << 20),
    )(row_order, gathered)


def square_on_device(n_seq, layer_inputs, out_grads, lengths, row_order, query_in, query_out):
    group = 4
    devices = n_seq * group
    seq_dev, seq_len, width_in = layer_inputs.shape
    flat_in = layer_inputs.reshape(seq_dev * seq_len, width_in)
    flat_out = out_grads.reshape(seq_dev * seq_len, out_grads.shape[2])
    axes = ("seq", "feat")
    first = [(s * group + f, s * group + (f ^ (1 if s % 2 == 0 else 2))) for s in range(n_seq) for f in range(group)]
    second = [(s * group + f, s * group + (f ^ (2 if s % 2 == 0 else 1))) for s in range(n_seq) for f in range(group)]
    feat = lax.axis_index("feat")
    odd = lax.axis_index("seq") % 2
    side = ((feat >> odd) & 1).astype(jnp.int32)
    keep, give = side[None], (1 - side)[None]

    def sized(half):
        def run():
            a_give = own_weights_matmul(give, lengths, flat_in, query_in, half)
            a_got = lax.ppermute(a_give, axes, first)
            b_give = half_matmul(give, lengths, flat_out, query_out, half)
            b_got = lax.ppermute(b_give, axes, first)
            a_keep = resident_matmul(keep, lengths, flat_in, query_in, half)
            a_pair = (a_keep.astype(jnp.float32) + a_got.astype(jnp.float32)).astype(jnp.bfloat16)
            a_far = lax.ppermute(a_pair, axes, second)
            b_keep = half_matmul(keep, lengths, flat_out, query_out, half)
            return partial_scores(keep, lengths, a_pair, a_far, b_keep, b_got, devices, tile_of(half, 384))

        return run

    total = seq_dev * seq_len
    halves = [total * k // 32 for k in SIXTEENTHS]
    packed = jnp.sum((lengths + GRAIN - 1) // GRAIN) * GRAIN
    which = sum((packed > 2 * half).astype(jnp.int32) for half in halves[:-1])
    mine = lax.switch(which, [sized(half) for half in halves])
    gathered = lax.all_to_all(mine, axes, 0, 0, tiled=True)
    return select_rows(row_order, gathered, group)


def on_device(layer_inputs, out_grads, lengths, row_order, query_in, query_out):
    seq_dev, seq_len, width_in = layer_inputs.shape
    total_rows = seq_dev * seq_len
    columns = query_in.shape[1]
    flat_in = layer_inputs.reshape(total_rows, width_in)
    flat_out = out_grads.reshape(total_rows, out_grads.shape[2])
    projected = lax.psum_scatter(
        jnp.concatenate(
            [
                jnp.dot(flat_in, query_in, preferred_element_type=jnp.float32),
                jnp.dot(flat_out, query_out, preferred_element_type=jnp.float32),
            ],
            axis=1,
        ).astype(jnp.bfloat16),
        "feat",
        scatter_dimension=0,
        tiled=True,
    ).astype(jnp.float32)
    first_row = lax.axis_index("feat") * projected.shape[0]
    row_count = projected.shape[0]
    products = projected[:, :columns] * projected[:, columns:]
    row_index = first_row + jnp.arange(row_count, dtype=jnp.int32)
    seq_owner = row_index // seq_len
    position = row_index % seq_len
    membership = (seq_owner[None, :] == jnp.arange(seq_dev, dtype=jnp.int32)[:, None]) & (
        position[None, :] < lengths[:, None]
    )
    seq_sums = jnp.dot(membership.astype(jnp.float32), products, precision=lax.Precision.HIGHEST)
    local_scores = seq_sums.reshape(seq_dev, Q, R).sum(axis=2)
    all_seqs = seq_dev * lax.axis_size("seq")
    placed = lax.dynamic_update_slice_in_dim(
        jnp.zeros((all_seqs, Q), jnp.float32), local_scores, lax.axis_index("seq") * seq_dev, 0
    )
    gathered = lax.psum(placed, ("seq", "feat"))
    selector = (row_order[:, None] == jnp.arange(all_seqs, dtype=jnp.int32)[None, :]).astype(
        jnp.float32
    )
    return jnp.dot(selector, gathered, precision=lax.Precision.HIGHEST)


def solution(mesh):
    n_seq, n_feat = mesh.shape["seq"], mesh.shape["feat"]
    body = functools.partial(square_on_device, n_seq) if n_feat == 4 and n_seq % 2 == 0 else on_device
    return jax.shard_map(
        body,
        mesh=mesh,
        in_specs=(
            P("seq", None, "feat"),
            P("seq", None, "feat"),
            P("seq"),
            P("seq"),
            P("feat", None),
            P("feat", None),
        ),
        out_specs=P("seq", None),
        check_vma=False,
    )
```
